32 devices in a mesh: lon: 8 (over z, core), lat: 4 (over y, x).
Axes of the slice: x: 2, y: 2, z: 4, core: 2. Of those that a mesh axis runs over, the one named last changes fastest.
Arguments:
- adjoint_state: float32 [4, 20, 256, 1024], P(None, None, 'lat', 'lon'), may hold values from -6 to 6
- coefficients: float32 [2, 256, 1024], P(None, 'lat', 'lon'), may hold values from 0.02 to 0.22
- mask: int32 [20, 256, 1024], P(None, 'lat', 'lon'), may hold values from 0 to 1, as said below
- bottom: int32 [256, 1024], P('lat', 'lon'), may hold values from 0 to 20, as said below
Outputs:
- sensitivity: float32 [4, 20, 256, 1024], P(None, None, 'lat', 'lon')
The draws below stay inside these ranges and needn't reach their ends.
Inputs may be any that keep to these rules, and one draw needn't show every extreme that they name: `mask`: 1 marks an ocean cell; a cell is 1 only at levels below its column's entry of bottom. `bottom`: levels reached by the column, 0 for land columns.
All inputs are finite; a program needn't handle non-finite values.
Results may differ from the reference program's by a relative error of at most 0.00002.
Values sent between devices are 32-bit elements; how exact they have to be, the bound alone decides.
A program may use at most 128 MiB of HBM per device.

```python
import jax
import jax.numpy as jnp
from jax import lax

LEV = 20
ITERS = 4
NY = 256
NX = 1024


def land_columns(key):
    base_key = jax.random.fold_in(key, 7)
    key_coarse, key_depth = jax.random.split(base_key)
    coarse = jax.random.randint(key_coarse, (NY // 8 + 1, NX // 8 + 1), 0, 10)
    land_flag = jnp.repeat(jnp.repeat(coarse, 8, axis=0), 8, axis=1)[:NY, :NX] < 3
    column_depth = jax.random.randint(key_depth, (NY, NX), LEV // 3 + 1, LEV + 1)
    return jnp.where(land_flag, 0, column_depth).astype(jnp.int32)


def draw_bottom(key, part):
    return land_columns(key)


def draw_mask(key, part):
    column_levels = land_columns(key)
    pocket_draw = jax.random.randint(jax.random.fold_in(key, 11), (LEV, NY, NX), 0, 10)
    level_ids = jnp.arange(LEV, dtype=jnp.int32)[:, None, None]
    return ((level_ids < column_levels[None]) & (pocket_draw != 0)).astype(jnp.int32)


def steps_of(stream_key, shape, shards, low, high):
    def one(axis_at, shards_of):
        heights = jax.random.uniform(jax.random.fold_in(jax.random.fold_in(stream_key, 6), axis_at), (shards_of,), jnp.float32, low / len(shards), high / len(shards))
        return jnp.repeat(jnp.exp(heights), shape[axis_at] // shards_of).reshape((-1,) + (1,) * (len(shape) - axis_at - 1))

    level = one(*shards[0])
    for cut in shards[1:]:
        level = level * one(*cut)
    return level


def scatter_about(stream_key, extent, scale, bound, cuts=(), kind=jnp.bfloat16):
    factor_of = steps_of(stream_key, extent, cuts, -0.22, 0.18) if cuts else 1.0
    values = jax.random.normal(stream_key, extent, jnp.float32) * scale * factor_of
    return jnp.minimum(jnp.maximum(values, -bound), bound).astype(kind)


def setup_inputs(seed: int = 0) -> dict:
    splits = jax.random.split(jax.random.key(seed), 5)
    adjoint_state = scatter_about(splits[0], (4, LEV, NY, NX), 1.0, 6.0, ((2, 4), (3, 8)), jnp.float32)
    coefficients = jnp.clip(0.02 + 0.2 * jax.random.uniform(splits[1], (2, NY, NX), jnp.float32) ** steps_of(splits[1], (2, NY, NX), ((1, 4), (2, 8)), -0.2, 0.2), 0.02, 0.22)
    mask = draw_mask(jax.random.fold_in(splits[4], 71), 0)
    bottom = draw_bottom(jax.random.fold_in(splits[4], 71), 0)
    return dict(adjoint_state=adjoint_state, coefficients=coefficients, mask=mask, bottom=bottom)


THERMAL_EXPANSION = 1.0
HALINE_CONTRACTION = 0.8
PRESSURE_SCALE = 0.05
BOTTOM_DRAG = 0.3
CORIOLIS_SCALE = 0.3


def neighbour_sum(field, fold_sign):
    east_side = jnp.roll(field, -1, -1)
    west_side = jnp.roll(field, 1, -1)
    north_side = jnp.concatenate([field[..., 1:, :], fold_sign * field[..., -1:, ::-1]], -2)
    south_side = jnp.concatenate([jnp.zeros_like(field[..., :1, :]), field[..., :-1, :]], -2)
    return east_side + west_side + north_side + south_side


def from_south(field):
    shifted = jnp.concatenate([jnp.zeros_like(field[..., :1, :]), field[..., :-1, :]], -2)
    mirrored = jnp.concatenate([jnp.zeros_like(field[..., :-1, :]), field[..., -1:, ::-1]], -2)
    return shifted + mirrored


def reference(adjoint_state, coefficients, mask, bottom):
    dtype = adjoint_state.dtype
    kappa = coefficients[0]
    viscosity = coefficients[1]
    row_values = jnp.arange(NY, dtype=jnp.int32).astype(dtype)
    coriolis = (CORIOLIS_SCALE * (2.0 * (row_values + 0.5) / NY - 1.0))[:, None]
    level_ids = jnp.arange(LEV, dtype=jnp.int32)
    drag_rate = BOTTOM_DRAG * (level_ids[:, None, None] == bottom[None] - 1).astype(dtype)
    wet_cell = mask.astype(dtype)
    tracer_keep = 1.0 - 4.0 * kappa

    def level_step(running, inputs):
        adjoint, wet_level, drag_level = inputs
        masked = wet_level[None] * adjoint
        momentum_keep = 1.0 - 4.0 * viscosity - drag_level
        temp_bar = tracer_keep * masked[0] + wet_level * neighbour_sum(kappa * masked[0], 1.0)
        salt_bar = tracer_keep * masked[1] + wet_level * neighbour_sum(kappa * masked[1], 1.0)
        zonal_bar = momentum_keep * masked[2] + wet_level * neighbour_sum(viscosity * masked[2], -1.0) - coriolis * masked[3]
        merid_bar = momentum_keep * masked[3] + wet_level * neighbour_sum(viscosity * masked[3], -1.0) + coriolis * masked[2]
        pressure_bar = masked[2] + masked[3] - jnp.roll(masked[2], 1, -1) - from_south(masked[3])
        running = running + PRESSURE_SCALE * pressure_bar
        temp_bar = temp_bar + wet_level * THERMAL_EXPANSION * running
        salt_bar = salt_bar - wet_level * HALINE_CONTRACTION * running
        return running, jnp.stack([temp_bar, salt_bar, zonal_bar, merid_bar])

    state = jnp.moveaxis(adjoint_state, 1, 0)
    for step_index in range(ITERS):
        start = jnp.zeros((NY, NX), dtype)
        _, state = lax.scan(level_step, start, (state, wet_cell, drag_rate), reverse=True)
    return jnp.moveaxis(state, 0, 1)
```

```python
import functools

import jax
import jax.numpy as jnp
from jax import lax
from jax.experimental import pallas as pl
from jax.experimental.pallas import tpu as pltpu
from jax.sharding import PartitionSpec as P

ITERS = 4
GROUPS = 2
CHUNK = 16
PAD = 8

HALINE_CONTRACTION = 0.8
PRESSURE_SCALE = 0.05
BOTTOM_DRAG = 0.3
CORIOLIS_SCALE = 0.3

KEEP, WEST, EAST, SOUTH, NORTH = range(5)


def kernel(
    n_lon, n_lat, levels, rows, cols, groups,
    state, coef, mask, bottom, out,
    buf, wet, mraw, bot, cf, stat, cor, top, rho, side, upper,
    csend, from_west, from_east, to_north, to_south, from_south, from_north,
    in_sem, out_sem, send_sem, recv_sem,
):
    per = levels // groups
    chunk = CHUNK
    lon, lat = lax.axis_index("lon"), lax.axis_index("lat")
    west, east = lax.rem(lon + n_lon - 1, n_lon), lax.rem(lon + 1, n_lon)
    is_top = lat == n_lat - 1
    not_top = lat < n_lat - 1
    not_low = lat > 0
    mirror = n_lon - 1 - lon

    def base(g):
        return levels - (g + 1) * per

    small = [
        pltpu.make_async_copy(coef, cf, in_sem.at[groups, 0]),
        pltpu.make_async_copy(bottom, bot, in_sem.at[groups, 1]),
    ]
    loads = [
        [
            pltpu.make_async_copy(
                state.at[:, pl.ds(base(g), per)],
                buf.at[0, :, pl.ds(base(g), per), pl.ds(PAD, rows), :],
                in_sem.at[g, 0],
            ),
            pltpu.make_async_copy(
                mask.at[pl.ds(base(g), per)], mraw.at[pl.ds(base(g), per)], in_sem.at[g, 1]
            ),
        ]
        for g in range(groups)
    ]
    for copy in small:
        copy.start()
    for pair in loads:
        for copy in pair:
            copy.start()

    barrier = pltpu.get_barrier_semaphore()

    def greet(target):
        pl.semaphore_signal(barrier, inc=1, device_id=target, device_id_type=pl.DeviceIdType.MESH)

    greet({"lon": west, "lat": lat})
    greet({"lon": east, "lat": lat})

    @pl.when(is_top)
    def _():
        greet({"lon": mirror, "lat": lat})

    @pl.when(not_top)
    def _():
        greet({"lon": lon, "lat": lat + 1})

    @pl.when(not_low)
    def _():
        greet({"lon": lon, "lat": lat - 1})

    pl.semaphore_wait(barrier, 3 + jnp.minimum(lat, 1))

    def remote(source, target, stage, g, sent, received, where):
        return pltpu.make_async_remote_copy(
            src_ref=source.at[stage, g],
            dst_ref=target.at[stage, g],
            send_sem=send_sem.at[stage, g, sent],
            recv_sem=recv_sem.at[stage, g, received],
            device_id=where,
            device_id_type=pl.DeviceIdType.MESH,
        )

    def go_west(stage, g):
        return remote(csend, from_east, stage, g, 0, 0, {"lon": west, "lat": lat})

    def go_east(stage, g):
        return remote(csend, from_west, stage, g, 1, 1, {"lon": east, "lat": lat})

    def go_north(stage, g):
        return remote(to_north, from_south, stage, g, 2, 2, {"lon": lon, "lat": lat + 1})

    def go_fold(stage, g):
        return remote(to_north, from_north, stage, g, 2, 3, {"lon": mirror, "lat": lat})

    def go_south(stage, g):
        return remote(to_south, from_north, stage, g, 3, 3, {"lon": lon, "lat": lat - 1})

    def send(stage, g):
        go_west(stage, g).start()
        go_east(stage, g).start()

        @pl.when(is_top)
        def _():
            go_fold(stage, g).start()

        @pl.when(not_top)
        def _():
            go_north(stage, g).start()

        @pl.when(not_low)
        def _():
            go_south(stage, g).start()

    def sent(stage, g):
        go_west(stage, g).wait_send()
        go_east(stage, g).wait_send()

        @pl.when(is_top)
        def _():
            go_fold(stage, g).wait_send()

        @pl.when(not_top)
        def _():
            go_north(stage, g).wait_send()

        @pl.when(not_low)
        def _():
            go_south(stage, g).wait_send()

    lane_c = lax.broadcasted_iota(jnp.int32, (chunk, cols), 1)
    half_c = lane_c >> 1
    first_lane, last_lane = lane_c == 0, lane_c == cols - 1

    def put(stage, g, j, r0, values):
        span = pl.ds(r0, chunk)
        packed = csend[stage, g, span, :]
        for f in range(4):
            fl = f * per + j
            packed = jnp.where(half_c == fl, pltpu.roll(values[f], 2 * fl + 1, 1), packed)
        csend[stage, g, span, :] = packed
        for f in range(4):
            fl = f * per + j
            if r0 == 0:
                to_south[stage, g, pl.ds(fl, 1), :] = values[f][0:1]
            if r0 + chunk == rows:
                to_north[stage, g, pl.ds(fl, 1), :] = values[f][chunk - 1 : chunk]

    csend[...] = jnp.zeros_like(csend)
    to_north[...] = jnp.zeros_like(to_north)
    to_south[...] = jnp.zeros_like(to_south)

    @pl.when(lat == 0)
    def _():
        from_south[...] = jnp.zeros_like(from_south)

    for copy in small:
        copy.wait()

    def settle(stage, g):
        go_west(stage, g).wait_recv()
        go_east(stage, g).wait_recv()
        go_fold(stage, g).wait_recv()

        @pl.when(not_low)
        def _():
            landed = remote(to_north, from_south, stage, g, 2, 2, {"lon": mirror, "lat": lat})
            landed.wait_recv()

        lane = lax.broadcasted_iota(jnp.int32, (rows, cols), 1)
        side[...] = jnp.where(
            (lane & 1) == 0, from_west[stage, g], pltpu.roll(from_east[stage, g], cols - 2, 1)
        )

        @pl.when(not_top)
        def _():
            upper[...] = from_north[stage, g]

        @pl.when(is_top)
        def _():
            line = from_north[stage, g]
            place = lax.broadcasted_iota(jnp.int32, line.shape, 1)
            item = lax.broadcasted_iota(jnp.int32, line.shape, 0)
            bit = 1
            while bit < cols:
                line = jnp.where(
                    (place & bit) == 0, pltpu.roll(line, cols - bit, 1), pltpu.roll(line, bit, 1)
                )
                bit *= 2
            flip = (item >= 2 * per) & (item < 4 * per)
            upper[...] = jnp.where(flip, -line, line)

    for g in range(groups):
        for copy in loads[g]:
            copy.wait()

        def first(i, carry, g=g):
            j = per - 1 - i
            level = base(g) + j
            for r0 in range(0, rows, chunk):
                w = mraw[level, pl.ds(r0, chunk), :].astype(jnp.float32)
                wet[level, pl.ds(r0, chunk), :] = w
                values = []
                for f in range(4):
                    t = w * buf[0, f, level, pl.ds(PAD + r0, chunk), :]
                    buf[0, f, level, pl.ds(PAD + r0, chunk), :] = t
                    values.append(t)
                put(0, g, j, r0, values)
            return carry

        lax.fori_loop(0, per, first, 0)
        if g == 0:
            for n in range(2):
                fl = 4 * per + n
                for r0 in range(0, rows, chunk):
                    packed = csend[0, 0, pl.ds(r0, chunk), :]
                    value = cf[n, pl.ds(r0, chunk), :]
                    csend[0, 0, pl.ds(r0, chunk), :] = jnp.where(
                        half_c == fl, pltpu.roll(value, 2 * fl + 1, 1), packed
                    )
                to_south[0, 0, fl : fl + 1, :] = cf[n, 0:1, :]
                to_north[0, 0, fl : fl + 1, :] = cf[n, rows - 1 : rows, :]
        send(0, g)

    row = lax.broadcasted_iota(jnp.int32, (rows, cols), 0)
    lane = lax.broadcasted_iota(jnp.int32, (rows, cols), 1)
    cor[...] = CORIOLIS_SCALE * (
        2.0 * ((lat * rows + row).astype(jnp.float32) + 0.5) / (n_lat * rows) - 1.0
    )
    top_device = jnp.where(is_top, 1.0, 0.0)
    top[...] = jnp.where(row == rows - 1, top_device, 0.0)
    bot[...] = bot[...] - 1

    for step in range(ITERS):
        cur, nxt = step % 2, (step + 1) % 2
        last = step == ITERS - 1
        rho[...] = jnp.zeros_like(rho)
        for g in range(groups):
            settle(step, g)
            if step == 0 and g == 0:
                for n in range(2):
                    fl = 4 * per + n
                    value = cf[n]
                    ends = pltpu.roll(side[...], cols - 2 * fl, 1)
                    stat[n, KEEP] = 1.0 - 4.0 * value
                    stat[n, WEST] = jnp.where(lane == 0, ends, pltpu.roll(value, 1, 1))
                    stat[n, EAST] = jnp.where(lane == cols - 1, ends, pltpu.roll(value, cols - 1, 1))
                    stat[n, SOUTH] = jnp.where(
                        row == 0, from_south[0, 0, fl : fl + 1, :], pltpu.roll(value, 1, 0)
                    )
                    stat[n, NORTH] = jnp.where(
                        row == rows - 1, upper[fl : fl + 1, :], pltpu.roll(value, rows - 1, 0)
                    )

            def advance(i, carry, g=g, step=step, cur=cur, nxt=nxt, last=last):
                j = per - 1 - i
                level = base(g) + j
                for f in range(4):
                    fl = f * per + j
                    buf[cur, f, level, PAD - 1 : PAD, :] = from_south[step, g, pl.ds(fl, 1), :]
                    buf[cur, f, level, PAD + rows : PAD + rows + 1, :] = upper[pl.ds(fl, 1), :]
                for r0 in range(0, rows, chunk):
                    span = pl.ds(r0, chunk)
                    edges = side[span, :]
                    here, near, wests, souths, norths = [], [], [], [], []
                    for f in range(4):
                        n = f // 2
                        fl = f * per + j
                        t = buf[cur, f, level, PAD + r0 : PAD + r0 + chunk, :]
                        ends = pltpu.roll(edges, lax.rem(cols - 2 * fl, cols), 1)
                        t_west = jnp.where(first_lane, ends, pltpu.roll(t, 1, 1))
                        t_east = jnp.where(last_lane, ends, pltpu.roll(t, cols - 1, 1))
                        t_south = buf[cur, f, level, PAD + r0 - 1 : PAD + r0 - 1 + chunk, :]
                        t_north = buf[cur, f, level, PAD + r0 + 1 : PAD + r0 + 1 + chunk, :]
                        near.append(
                            stat[n, WEST, span, :] * t_west
                            + stat[n, EAST, span, :] * t_east
                            + stat[n, SOUTH, span, :] * t_south
                            + stat[n, NORTH, span, :] * t_north
                        )
                        here.append(t)
                        wests.append(t_west)
                        souths.append(t_south)
                        norths.append(t_north)
                    q = here[2] + here[3] - wests[2] - souths[3]
                    if r0 + chunk == rows:
                        q = q + top[span, :] * norths[3]
                    run = rho[span, :] + PRESSURE_SCALE * q
                    rho[span, :] = run
                    w = wet[level, span, :]
                    keep = stat[0, KEEP, span, :]
                    drag = jnp.where(bot[span, :] == level, BOTTOM_DRAG, 0.0)
                    keep_uv = stat[1, KEEP, span, :] - drag
                    c = cor[span, :]
                    values = [
                        w * (keep * here[0] + near[0] + run),
                        w * (keep * here[1] + near[1] - HALINE_CONTRACTION * run),
                        w * (keep_uv * here[2] + near[2] - c * here[3]),
                        w * (keep_uv * here[3] + near[3] + c * here[2]),
                    ]
                    for f in range(4):
                        buf[nxt, f, level, PAD + r0 : PAD + r0 + chunk, :] = values[f]
                    if not last:
                        put(step + 1, g, j, r0, values)
                return carry

            lax.fori_loop(0, per, advance, 0)
            if not last:
                send(step + 1, g)
            else:
                store(out, buf, out_sem, nxt, base(g), per, rows, g).start()

    for stage in range(ITERS):
        for g in range(groups):
            sent(stage, g)
    for g in range(groups):
        store(out, buf, out_sem, ITERS % 2, base(g), per, rows, g).wait()


def store(out, buf, out_sem, slot, base, per, rows, g):
    return pltpu.make_async_copy(
        buf.at[slot, :, pl.ds(base, per), pl.ds(PAD, rows), :],
        out.at[:, pl.ds(base, per)],
        out_sem.at[g],
    )


def solution(mesh):
    n_lon, n_lat = mesh.shape["lon"], mesh.shape["lat"]
    placed = (
        P(None, None, "lat", "lon"),
        P(None, "lat", "lon"),
        P(None, "lat", "lon"),
        P("lat", "lon"),
    )

    def local(adjoint_state, coefficients, mask, bottom):
        levels, rows, cols = mask.shape
        groups = GROUPS
        per = levels // groups
        lines = -(-(4 * per + 2) // 8) * 8
        f32 = jnp.float32
        dma = pltpu.SemaphoreType.DMA
        return pl.pallas_call(
            functools.partial(kernel, n_lon, n_lat, levels, rows, cols, groups),
            out_shape=jax.ShapeDtypeStruct(adjoint_state.shape, f32),
            in_specs=[pl.BlockSpec(memory_space=pl.ANY)] * 4,
            out_specs=pl.BlockSpec(memory_space=pl.ANY),
            scratch_shapes=[
                pltpu.VMEM((2, 4, levels, rows + 2 * PAD, cols), f32),
                pltpu.VMEM((levels, rows, cols), f32),
                pltpu.VMEM((levels, rows, cols), jnp.int32),
                pltpu.VMEM((rows, cols), jnp.int32),
                pltpu.VMEM((2, rows, cols), f32),
                pltpu.VMEM((2, 5, rows, cols), f32),
                pltpu.VMEM((rows, cols), f32),
                pltpu.VMEM((rows, cols), f32),
                pltpu.VMEM((rows, cols), f32),
                pltpu.VMEM((rows, cols), f32),
                pltpu.VMEM((lines, cols), f32),
                pltpu.VMEM((ITERS, groups, rows, cols), f32),
                pltpu.VMEM((ITERS, groups, rows, cols), f32),
                pltpu.VMEM((ITERS, groups, rows, cols), f32),
                pltpu.VMEM((ITERS, groups, lines, cols), f32),
                pltpu.VMEM((ITERS, groups, lines, cols), f32),
                pltpu.VMEM((ITERS, groups, lines, cols), f32),
                pltpu.VMEM((ITERS, groups, lines, cols), f32),
                dma((groups + 1, 2)),
                dma((groups,)),
                dma((ITERS, groups, 4)),
                dma((ITERS, groups, 4)),
            ],
            compiler_params=pltpu.CompilerParams(
                collective_id=0, has_side_effects=True, vmem_limit_bytes=40 << 20
            ),
            name="adjoint_steps",
        )(adjoint_state, coefficients, mask, bottom)

    return jax.shard_map(
        local, mesh=mesh, in_specs=placed, out_specs=P(None, None, "lat", "lon"), check_vma=False
    )
```

```python
import functools

import jax
import jax.numpy as jnp
from jax import lax
from jax.experimental import pallas as pl
from jax.experimental.pallas import tpu as pltpu
from jax.sharding import PartitionSpec as P

ITERS = 4
GROUPS = 4
CHUNK = 16
PAD = 8

HALINE_CONTRACTION = 0.8
PRESSURE_SCALE = 0.05
BOTTOM_DRAG = 0.3
CORIOLIS_SCALE = 0.3

KEEP, WEST, EAST, SOUTH, NORTH = range(5)


def kernel(
    n_lon, n_lat, levels, rows, cols, groups,
    state, coef, mask, bottom, out,
    buf_a, buf_b, wet, mraw, bot, cf, stat, cor, top, rho, side, upper,
    csend, from_west, from_east, to_north, to_south, from_south, from_north,
    in_sem, out_sem, send_sem, recv_sem,
):
    per = levels // groups
    chunk = CHUNK
    bufs = (buf_a, buf_b)
    lon, lat = lax.axis_index("lon"), lax.axis_index("lat")
    west, east = lax.rem(lon + n_lon - 1, n_lon), lax.rem(lon + 1, n_lon)
    is_top = lat == n_lat - 1
    not_top = lat < n_lat - 1
    not_low = lat > 0
    mirror = n_lon - 1 - lon

    def base(g):
        return levels - (g + 1) * per

    small = [
        pltpu.make_async_copy(coef, cf, in_sem.at[groups, 0]),
        pltpu.make_async_copy(bottom, bot, in_sem.at[groups, 1]),
    ]

    def load(g):
        return [
            pltpu.make_async_copy(
                state.at[:, pl.ds(base(g), per)],
                bufs[0].at[:, pl.ds(base(g), per), pl.ds(PAD, rows), :],
                in_sem.at[g, 0],
            ),
            pltpu.make_async_copy(
                mask.at[pl.ds(base(g), per)], mraw.at[pl.ds(base(g), per)], in_sem.at[g, 1]
            ),
        ]

    for copy in small:
        copy.start()
    for g in range(groups):
        for copy in load(g):
            copy.start()

    barrier = pltpu.get_barrier_semaphore()

    def greet(target):
        pl.semaphore_signal(barrier, inc=1, device_id=target, device_id_type=pl.DeviceIdType.MESH)

    greet({"lon": west, "lat": lat})
    greet({"lon": east, "lat": lat})

    @pl.when(is_top)
    def _():
        greet({"lon": mirror, "lat": lat})

    @pl.when(not_top)
    def _():
        greet({"lon": lon, "lat": lat + 1})

    @pl.when(not_low)
    def _():
        greet({"lon": lon, "lat": lat - 1})

    pl.semaphore_wait(barrier, 3 + jnp.minimum(lat, 1))

    def remote(source, target, stage, g, sent, received, where):
        return pltpu.make_async_remote_copy(
            src_ref=source.at[stage, g],
            dst_ref=target.at[stage, g],
            send_sem=send_sem.at[stage, g, sent],
            recv_sem=recv_sem.at[stage, g, received],
            device_id=where,
            device_id_type=pl.DeviceIdType.MESH,
        )

    def go_west(stage, g):
        return remote(csend, from_east, stage, g, 0, 0, {"lon": west, "lat": lat})

    def go_east(stage, g):
        return remote(csend, from_west, stage, g, 1, 1, {"lon": east, "lat": lat})

    def go_north(stage, g):
        return remote(to_north, from_south, stage, g, 2, 2, {"lon": lon, "lat": lat + 1})

    def go_fold(stage, g):
        return remote(to_north, from_north, stage, g, 2, 3, {"lon": mirror, "lat": lat})

    def go_south(stage, g):
        return remote(to_south, from_north, stage, g, 3, 3, {"lon": lon, "lat": lat - 1})

    def send(stage, g):
        go_west(stage, g).start()
        go_east(stage, g).start()

        @pl.when(is_top)
        def _():
            go_fold(stage, g).start()

        @pl.when(not_top)
        def _():
            go_north(stage, g).start()

        @pl.when(not_low)
        def _():
            go_south(stage, g).start()

    def sent(stage, g):
        go_west(stage, g).wait_send()
        go_east(stage, g).wait_send()

        @pl.when(is_top)
        def _():
            go_fold(stage, g).wait_send()

        @pl.when(not_top)
        def _():
            go_north(stage, g).wait_send()

        @pl.when(not_low)
        def _():
            go_south(stage, g).wait_send()

    lane_c = lax.broadcasted_iota(jnp.int32, (chunk, cols), 1)
    half_c = lane_c >> 1
    first_lane, last_lane = lane_c == 0, lane_c == cols - 1

    def put(stage, g, j, r0, values):
        span = pl.ds(r0, chunk)
        packed = csend[stage, g, span, :]
        for f in range(4):
            fl = f * per + j
            packed = jnp.where(half_c == fl, pltpu.roll(values[f], 2 * fl + 1, 1), packed)
        csend[stage, g, span, :] = packed
        for f in range(4):
            fl = f * per + j
            if r0 == 0:
                to_south[stage, g, pl.ds(fl, 1), :] = values[f][0:1]
            if r0 + chunk == rows:
                to_north[stage, g, pl.ds(fl, 1), :] = values[f][chunk - 1 : chunk]

    csend[...] = jnp.zeros_like(csend)
    to_north[...] = jnp.zeros_like(to_north)
    to_south[...] = jnp.zeros_like(to_south)

    @pl.when(lat == 0)
    def _():
        from_south[...] = jnp.zeros_like(from_south)

    for copy in small:
        copy.wait()

    def settle(stage, g):
        go_west(stage, g).wait_recv()
        go_east(stage, g).wait_recv()
        go_fold(stage, g).wait_recv()

        @pl.when(not_low)
        def _():
            landed = remote(to_north, from_south, stage, g, 2, 2, {"lon": mirror, "lat": lat})
            landed.wait_recv()

        lane = lax.broadcasted_iota(jnp.int32, (rows, cols), 1)
        side[...] = jnp.where(
            (lane & 1) == 0, from_west[stage, g], pltpu.roll(from_east[stage, g], cols - 2, 1)
        )

        @pl.when(not_top)
        def _():
            upper[...] = from_north[stage, g]

        @pl.when(is_top)
        def _():
            line = from_north[stage, g]
            item = lax.broadcasted_iota(jnp.int32, line.shape, 0)
            place = cols - 1 - lax.broadcasted_iota(jnp.int32, line.shape, 1)
            line = jnp.take_along_axis(line, place, axis=1, mode="promise_in_bounds")
            flip = (item >= 2 * per) & (item < 4 * per)
            upper[...] = jnp.where(flip, -line, line)

    def begin(g, carry):
        for copy in load(g):
            copy.wait()

        def first(i, carry):
            j = per - 1 - i
            level = base(g) + j
            for r0 in range(0, rows, chunk):
                w = mraw[level, pl.ds(r0, chunk), :].astype(jnp.float32)
                wet[level, pl.ds(r0, chunk), :] = w
                values = []
                for f in range(4):
                    t = w * bufs[0][f, level, pl.ds(PAD + r0, chunk), :]
                    bufs[0][f, level, pl.ds(PAD + r0, chunk), :] = t
                    values.append(t)
                put(0, g, j, r0, values)
            return carry

        lax.fori_loop(0, per, first, 0)

        @pl.when(g == 0)
        def _():
            for n in range(2):
                fl = 4 * per + n
                for r0 in range(0, rows, chunk):
                    packed = csend[0, 0, pl.ds(r0, chunk), :]
                    value = cf[n, pl.ds(r0, chunk), :]
                    csend[0, 0, pl.ds(r0, chunk), :] = jnp.where(
                        half_c == fl, pltpu.roll(value, 2 * fl + 1, 1), packed
                    )
                to_south[0, 0, fl : fl + 1, :] = cf[n, 0:1, :]
                to_north[0, 0, fl : fl + 1, :] = cf[n, rows - 1 : rows, :]

        send(0, g)
        return carry

    lax.fori_loop(0, groups, begin, 0)

    row = lax.broadcasted_iota(jnp.int32, (rows, cols), 0)
    lane = lax.broadcasted_iota(jnp.int32, (rows, cols), 1)
    cor[...] = CORIOLIS_SCALE * (
        2.0 * ((lat * rows + row).astype(jnp.float32) + 0.5) / (n_lat * rows) - 1.0
    )
    top_device = jnp.where(is_top, 1.0, 0.0)
    top[...] = jnp.where(row == rows - 1, top_device, 0.0)
    bot[...] = bot[...] - 1

    def weigh():
        for n in range(2):
            fl = 4 * per + n
            value = cf[n]
            ends = pltpu.roll(side[...], cols - 2 * fl, 1)
            stat[n, KEEP] = 1.0 - 4.0 * value
            stat[n, WEST] = jnp.where(lane == 0, ends, pltpu.roll(value, 1, 1))
            stat[n, EAST] = jnp.where(lane == cols - 1, ends, pltpu.roll(value, cols - 1, 1))
            stat[n, SOUTH] = jnp.where(
                row == 0, from_south[0, 0, fl : fl + 1, :], pltpu.roll(value, 1, 0)
            )
            stat[n, NORTH] = jnp.where(
                row == rows - 1, upper[fl : fl + 1, :], pltpu.roll(value, rows - 1, 0)
            )

    def turn(step, g, carry):
        cur, nxt = bufs[step % 2], bufs[(step + 1) % 2]
        last = step == ITERS - 1
        settle(step, g)

        if step == 0:

            @pl.when(g == 0)
            def _():
                weigh()

        @pl.when(g == 0)
        def _():
            rho[...] = jnp.zeros_like(rho)

        def advance(i, carry):
            j = per - 1 - i
            level = base(g) + j
            for f in range(4):
                fl = f * per + j
                cur[f, level, PAD - 1 : PAD, :] = from_south[step, g, pl.ds(fl, 1), :]
                cur[f, level, PAD + rows : PAD + rows + 1, :] = upper[pl.ds(fl, 1), :]
            for r0 in range(0, rows, chunk):
                span = pl.ds(r0, chunk)
                edges = side[span, :]
                here, near, wests, souths, norths = [], [], [], [], []
                for f in range(4):
                    n = f // 2
                    fl = f * per + j
                    t = cur[f, level, PAD + r0 : PAD + r0 + chunk, :]
                    ends = pltpu.roll(edges, lax.rem(cols - 2 * fl, cols), 1)
                    t_west = jnp.where(first_lane, ends, pltpu.roll(t, 1, 1))
                    t_east = jnp.where(last_lane, ends, pltpu.roll(t, cols - 1, 1))
                    t_south = cur[f, level, PAD + r0 - 1 : PAD + r0 - 1 + chunk, :]
                    t_north = cur[f, level, PAD + r0 + 1 : PAD + r0 + 1 + chunk, :]
                    near.append(
                        stat[n, WEST, span, :] * t_west
                        + stat[n, EAST, span, :] * t_east
                        + stat[n, SOUTH, span, :] * t_south
                        + stat[n, NORTH, span, :] * t_north
                    )
                    here.append(t)
                    wests.append(t_west)
                    souths.append(t_south)
                    norths.append(t_north)
                q = here[2] + here[3] - wests[2] - souths[3]
                if r0 + chunk == rows:
                    q = q + top[span, :] * norths[3]
                run = rho[span, :] + PRESSURE_SCALE * q
                rho[span, :] = run
                w = wet[level, span, :]
                keep = stat[0, KEEP, span, :]
                drag = jnp.where(bot[span, :] == level, BOTTOM_DRAG, 0.0)
                keep_uv = stat[1, KEEP, span, :] - drag
                c = cor[span, :]
                values = [
                    w * (keep * here[0] + near[0] + run),
                    w * (keep * here[1] + near[1] - HALINE_CONTRACTION * run),
                    w * (keep_uv * here[2] + near[2] - c * here[3]),
                    w * (keep_uv * here[3] + near[3] + c * here[2]),
                ]
                for f in range(4):
                    nxt[f, level, PAD + r0 : PAD + r0 + chunk, :] = values[f]
                if not last:
                    put(step + 1, g, j, r0, values)
            return carry

        lax.fori_loop(0, per, advance, 0)
        if not last:
            send(step + 1, g)
        else:
            store(out, nxt, out_sem, base(g), per, rows, g).start()
        return carry

    for step in range(ITERS):
        lax.fori_loop(0, groups, functools.partial(turn, step), 0)

    def drain(m, carry):
        sent(m // groups, m % groups)
        return carry

    lax.fori_loop(0, ITERS * groups, drain, 0)
    for g in range(groups):
        store(out, bufs[ITERS % 2], out_sem, base(g), per, rows, g).wait()


def store(out, buf, out_sem, base, per, rows, g):
    return pltpu.make_async_copy(
        buf.at[:, pl.ds(base, per), pl.ds(PAD, rows), :],
        out.at[:, pl.ds(base, per)],
        out_sem.at[g],
    )


def solution(mesh):
    n_lon, n_lat = mesh.shape["lon"], mesh.shape["lat"]
    placed = (
        P(None, None, "lat", "lon"),
        P(None, "lat", "lon"),
        P(None, "lat", "lon"),
        P("lat", "lon"),
    )

    def local(adjoint_state, coefficients, mask, bottom):
        levels, rows, cols = mask.shape
        groups = GROUPS
        per = levels // groups
        lines = -(-(4 * per + 2) // 8) * 8
        f32 = jnp.float32
        dma = pltpu.SemaphoreType.DMA
        return pl.pallas_call(
            functools.partial(kernel, n_lon, n_lat, levels, rows, cols, groups),
            out_shape=jax.ShapeDtypeStruct(adjoint_state.shape, f32),
            in_specs=[pl.BlockSpec(memory_space=pl.ANY)] * 4,
            out_specs=pl.BlockSpec(memory_space=pl.ANY),
            scratch_shapes=[
                pltpu.VMEM((4, levels, rows + 2 * PAD, cols), f32),
                pltpu.VMEM((4, levels, rows + 2 * PAD, cols), f32),
                pltpu.VMEM((levels, rows, cols), f32),
                pltpu.VMEM((levels, rows, cols), jnp.int32),
                pltpu.VMEM((rows, cols), jnp.int32),
                pltpu.VMEM((2, rows, cols), f32),
                pltpu.VMEM((2, 5, rows, cols), f32),
                pltpu.VMEM((rows, cols), f32),
                pltpu.VMEM((rows, cols), f32),
                pltpu.VMEM((rows, cols), f32),
                pltpu.VMEM((rows, cols), f32),
                pltpu.VMEM((lines, cols), f32),
                pltpu.VMEM((ITERS, groups, rows, cols), f32),
                pltpu.VMEM((ITERS, groups, rows, cols), f32),
                pltpu.VMEM((ITERS, groups, rows, cols), f32),
                pltpu.VMEM((ITERS, groups, lines, cols), f32),
                pltpu.VMEM((ITERS, groups, lines, cols), f32),
                pltpu.VMEM((ITERS, groups, lines, cols), f32),
                pltpu.VMEM((ITERS, groups, lines, cols), f32),
                dma((groups + 1, 2)),
                dma((groups,)),
                dma((ITERS, groups, 4)),
                dma((ITERS, groups, 4)),
            ],
            compiler_params=pltpu.CompilerParams(
                collective_id=0, has_side_effects=True, vmem_limit_bytes=60 << 20
            ),
            name="adjoint_steps",
        )(adjoint_state, coefficients, mask, bottom)

    return jax.shard_map(
        local, mesh=mesh, in_specs=placed, out_specs=P(None, None, "lat", "lon"), check_vma=False
    )
```
